32 devices in a mesh: grp: 2 (over x), gx: 4 (over z), gz: 4 (over y, core).
Axes of the slice: x: 2, y: 2, z: 4, core: 2. Of those that a mesh axis runs over, the one named last changes fastest.
Arguments:
- primal: float32 [2, 3, 128, 2048], P(None, None, 'gx', ('gz', 'grp')), may hold values from -6 to 6
- tangent: float32 [16, 128, 2048], P('grp', 'gx', 'gz'), may hold values from -6 to 6
- diffusion: float32 [128, 2048], P('gx', 'gz'), may hold values from 0.05 to 0.5
Outputs:
- basis: float32 [16, 128, 2048], P('grp', 'gx', 'gz')
- factor: float32 [16, 16], replicated
The draws below stay inside these ranges and needn't reach their ends.
All inputs are finite; a program needn't handle non-finite values.
Results may differ from the reference program's by a relative error of at most 0.000098.
Values sent between devices are 32-bit elements; how exact they have to be, the bound alone decides.
A program may use at most 64 MiB of HBM per device.

```python
import math
import jax
import jax.numpy as jnp
from jax import lax

DIRS = 16
STEPS = 2
NX = 128
NZ = 2048


def steps_of(key, extent, pieces, smallest, largest):
    gain, own = 1.0, jax.random.fold_in(key, 6)
    for axis_at, parts in pieces:
        heights = jnp.exp(jax.random.uniform(jax.random.fold_in(own, axis_at), (parts,), jnp.float32, smallest / len(pieces), largest / len(pieces)))
        gain = gain * jnp.repeat(heights, extent[axis_at] // parts).reshape([-1 if axis == axis_at else 1 for axis in range(len(extent))])
    return gain


def normal_values(own_key, dims, scale, limit, pieces=(), kind=jnp.bfloat16):
    drawn = scale * jax.random.normal(own_key, dims, jnp.float32)
    if pieces:
        drawn = drawn * steps_of(own_key, dims, pieces, -0.22, 0.18)
    return jnp.clip(drawn, -limit, limit).astype(kind)


def setup_inputs(seed: int = 0) -> dict:
    keys = jax.random.split(jax.random.key(seed), 4)
    primal = normal_values(keys[0], (STEPS, 3, NX, NZ), 1.0, 6.0, ((2, 4), (3, 8)), jnp.float32)
    tangent = normal_values(keys[1], (DIRS, NX, NZ), 1.0, 6.0, ((0, 2), (1, 4), (2, 4)), jnp.float32)
    diffusion = jnp.clip(jnp.exp(math.log(0.5) - 2.3025851 * jax.random.uniform(keys[2], (NX, NZ), jnp.float32) ** steps_of(keys[2], (NX, NZ), ((0, 4), (1, 4)), -0.2, 0.2)), 0.05, 0.5)
    return {"primal": primal, "tangent": tangent, "diffusion": diffusion}


time_step = 0.25

def advance(tangent, velocity, diffusion):
    to_east = jnp.roll(tangent, -1, axis=1)
    to_west = jnp.roll(tangent, 1, axis=1)
    to_north = jnp.roll(tangent, -1, axis=2)
    to_south = jnp.roll(tangent, 1, axis=2)
    change = -velocity[0] * (to_east - to_west) * 0.5 - velocity[1] * (to_north - to_south) * 0.5 + diffusion * (to_east + to_west + to_north + to_south - 4.0 * tangent) - velocity[2] * tangent
    return tangent + time_step * change

def reference(primal, tangent, diffusion):
    for step in range(STEPS):
        tangent = advance(tangent, primal[step], diffusion)
    flattened = tangent.reshape(DIRS, -1)
    gram_matrix = jnp.dot(flattened, flattened.T, precision=lax.Precision.HIGHEST) / (NX * NZ)
    lower = jnp.linalg.cholesky(gram_matrix)
    basis = jax.scipy.linalg.solve_triangular(lower, flattened, lower=True).reshape(tangent.shape)
    return (basis, lower.T)
```

```python
import functools
import jax
import jax.numpy as jnp
from jax import lax
from jax.experimental import pallas as pl
from jax.experimental.pallas import tpu as pltpu
from jax.sharding import PartitionSpec as P

time_step = 0.25
LANES = 128
BLOCK = 8
MESH = pl.DeviceIdType.MESH
HIGHEST = lax.Precision.HIGHEST


def coefficients(velocity, diffusion):
    half_u = 0.5 * velocity[0]
    half_v = 0.5 * velocity[1]
    return (
        time_step * (diffusion - half_u),
        time_step * (diffusion + half_u),
        time_step * (diffusion - half_v),
        time_step * (diffusion + half_v),
        1.0 - time_step * (4.0 * diffusion + velocity[2]),
    )


def kernel(groups, ranks, spans, primal, tangent, diffusion, out, factor,
           mine, land, prim, diff, row_send, row_land, col_send, col_land, comb,
           vcol_send, vcol_land, vrow_send, vrow_land,
           field, first, coef0, coef1, advanced, gram1, gram2, result,
           load_sem, raw_send, raw_recv, rs_send, rs_recv, cs_send, cs_recv,
           vc_send, vc_recv, vr_send, vr_recv, g1_send, g1_recv, g2_send, g2_recv,
           fin_send, fin_recv):
    own, rows, columns = out.shape
    width = columns // groups
    tiles = width // LANES
    dirs = own * groups
    blocks = rows // BLOCK
    wide = width + LANES
    cells = rows * columns * ranks * spans
    g, x, z = lax.axis_index("grp"), lax.axis_index("gx"), lax.axis_index("gz")

    def dev(a, b, c):
        return {"grp": a, "gx": b, "gz": c}

    def up(i, k, n):
        return lax.rem(i + k + n, n)

    loads = []
    for t in range(groups * tiles):
        loads.append(pltpu.make_async_copy(
            tangent.at[:, pl.ds(t * LANES, LANES)], mine.at[t], load_sem.at[t]))
    base = groups * tiles
    loads.append(pltpu.make_async_copy(primal, prim, load_sem.at[base]))
    loads.append(pltpu.make_async_copy(
        diffusion.at[:, pl.ds(pl.multiple_of(g * width, LANES), width)], diff, load_sem.at[base + 1]))
    for t in range(tiles):
        loads.append(pltpu.make_async_copy(
            tangent.at[:, pl.ds(pl.multiple_of(g * width + t * LANES, LANES), LANES)],
            land.at[t, pl.ds(pl.multiple_of(g * own * rows, 8), own * rows), :], load_sem.at[base + 2 + t]))
    for copy in loads:
        copy.start()

    barrier = pltpu.get_barrier_semaphore()
    greeted = set()
    for dg in range(groups):
        for dx in (-1, 0, 1):
            for dz in (-1, 0, 1):
                greeted.add((dg, dx % ranks, dz % spans))
        for dz in range(spans):
            greeted.add((dg, 0, dz))
    for dx in range(ranks):
        greeted.add((0, dx, 0))
    greeted.discard((0, 0, 0))
    for dg, dx, dz in sorted(greeted):
        pl.semaphore_signal(barrier, inc=1, device_id=dev(up(g, dg, groups), up(x, dx, ranks), up(z, dz, spans)),
                            device_id_type=MESH)
    pl.semaphore_wait(barrier, len(greeted))

    def send(src, dst, s_sem, r_sem, to):
        copy = pltpu.make_async_remote_copy(src_ref=src, dst_ref=dst, send_sem=s_sem, recv_sem=r_sem,
                                            device_id=to, device_id_type=MESH)
        copy.start()
        return copy

    raw_copies = []
    for k in range(1, groups):
        p = up(g, k, groups)
        for t in range(tiles):
            raw_copies.append(send(
                tangent.at[:, pl.ds(pl.multiple_of(p * width + t * LANES, LANES), LANES)],
                land.at[t, pl.ds(pl.multiple_of(g * own * rows, 8), own * rows), :],
                raw_send.at[k, t], raw_recv.at[k, t], dev(p, x, z)))

    for copy in loads[:base + 2]:
        copy.wait()

    lane = lax.broadcasted_iota(jnp.int32, (own, LANES), 1)
    per_tile = LANES // 4
    col_tiles = -(-rows // per_tile)
    for j in range(groups):
        for c in range(col_tiles):
            acc = jnp.zeros((own, LANES), jnp.float32)
            for r in range(c * per_tile, min(rows, (c + 1) * per_tile)):
                edge = mine[j * tiles, pl.ds(r, own, stride=rows), :]
                if tiles > 1:
                    edge = jnp.where(lane < LANES // 2, edge,
                                     mine[j * tiles + tiles - 1, pl.ds(r, own, stride=rows), :])
                shift = 4 * (r - c * per_tile)
                if shift:
                    edge = pltpu.roll(edge, shift, 1)
                acc = jnp.where(((lane + (LANES + 2 - shift)) % LANES) < 4, edge, acc)
            col_send[j, c] = acc
    for side, picks in ((0, (0, 1)), (1, (rows - 2, rows - 1))):
        for j in range(groups):
            for i, r in enumerate(picks):
                for t in range(tiles):
                    row_send[side, j, i, :, t * LANES:(t + 1) * LANES] = mine[
                        j * tiles + t, pl.ds(r, own, stride=rows), :]
    for side, r in ((0, 0), (1, rows - 1)):
        for f in range(3):
            vrow_send[side, f:f + 1, :] = prim[0, f, r:r + 1, :]
        vrow_send[side, 3:4, :] = diff[r:r + 1, :]
        vrow_send[side, 4:8, :] = jnp.zeros((4, width), jnp.float32)
    vlane = lax.broadcasted_iota(jnp.int32, (rows, LANES), 1)
    left_acc = jnp.zeros((rows, LANES), jnp.float32)
    right_acc = jnp.zeros((rows, LANES), jnp.float32)
    for f in range(4):
        whole_field = prim[0, f] if f < 3 else diff[...]
        left = whole_field[:, :LANES]
        right = whole_field[:, width - LANES:]
        if f:
            left = pltpu.roll(left, f, 1)
            right = pltpu.roll(right, LANES - f, 1)
        left_acc = jnp.where(vlane == f, left, left_acc)
        right_acc = jnp.where(vlane == LANES - 1 - f, right, right_acc)
    vcol_send[0] = left_acc
    vcol_send[1] = right_acc

    row_copies = []
    for side, dx in ((0, -1), (1, 1)):
        for k in range(groups):
            p = up(g, k, groups)
            row_copies.append(send(row_send.at[side, p], row_land.at[side, g], rs_send.at[side, k],
                                   rs_recv.at[side, k], dev(p, up(x, dx, ranks), z)))
        row_copies.append(send(vrow_send.at[side], vrow_land.at[side], vr_send.at[side], vr_recv.at[side],
                               dev(g, up(x, dx, ranks), z)))
    chunk = z * groups + g
    chunks = spans * groups
    for side, step in ((0, -1), (1, 1)):
        to = up(chunk, step, chunks)
        row_copies.append(send(vcol_send.at[side], vcol_land.at[side], vc_send.at[side], vc_recv.at[side],
                               dev(lax.rem(to, groups), x, lax.div(to, groups))))
    for dx in (-1, 1, 0):
        slot = 1 - dx
        for j in range(groups):
            for side, step in ((0, -1), (1, 1)):
                dg = (j + step) % groups
                inside = 0 <= j + step < groups
                dz = z if inside else up(z, step, spans)

                def issue(j=j, side=side, dg=dg, dz=dz, slot=slot, dx=dx):
                    send(col_send.at[j], col_land.at[slot, side, g], cs_send.at[slot, side, j],
                         cs_recv.at[slot, side, g], dev(dg, up(x, dx, ranks), dz))
                if inside and dx == 0:
                    pl.when(g != dg)(issue)

                    @pl.when(g == dg)
                    def _(j=j, side=side, dg=dg, slot=slot):
                        col_land[slot, side, dg] = col_send[j]
                else:
                    issue()
    for i, value in enumerate(coefficients([prim[1, f] for f in range(3)], diff[...])):
        coef1[i] = value

    for copy in row_copies:
        copy.wait_recv()
    halo = []
    for f in range(4):
        after, before = vcol_land[0], vcol_land[1]
        if f:
            after = pltpu.roll(after, LANES - f, 1)
            before = pltpu.roll(before, f, 1)
        halo.append(jnp.where(vlane < LANES // 2, after, before))
    for i, value in enumerate(coefficients([prim[0, f] for f in range(3)], diff[...])):
        coef0[i, BLOCK:BLOCK + rows, :width] = value
    for i, value in enumerate(coefficients(halo[:3], halo[3])):
        coef0[i, BLOCK:BLOCK + rows, width:] = value
    for side, at in ((0, BLOCK + rows), (1, BLOCK - 1)):
        part = [vrow_land[side, f:f + 1, :] for f in range(4)]
        for i, value in enumerate(coefficients(part[:3], part[3])):
            coef0[i, at:at + 1, :width] = value
            coef0[i, at:at + 1, width:] = jnp.zeros((1, LANES), jnp.float32)

    for side, at in ((0, rows + 2), (1, 0)):
        for s in range(groups):
            for i in range(2):
                field[at + i, s * own:(s + 1) * own, :width] = row_land[side, s, i]

    other = dev(up(g, 1, groups), x, z)
    for slot in range(3):
        for side in range(2):
            for s in range(groups):
                def arrived(slot=slot, side=side, s=s):
                    pltpu.make_async_remote_copy(
                        src_ref=col_send.at[0], dst_ref=col_land.at[slot, side, s],
                        send_sem=cs_send.at[slot, side, 0], recv_sem=cs_recv.at[slot, side, s],
                        device_id=other, device_id_type=MESH).wait_recv()
                if slot == 1:
                    inside = (g < groups - 1) if side == 0 else (g > 0)
                    pl.when(jnp.logical_not(jnp.logical_and(inside, g == s)))(arrived)
                else:
                    arrived()
    for slot in range(3):
        for c in range(col_tiles):
            for s in range(groups):
                comb[slot, c, s * own:(s + 1) * own, :] = jnp.where(
                    lane % 4 < 2, col_land[slot, 0, s, c], col_land[slot, 1, s, c])

    def edge_tile(slot, r):
        shift = 4 * (r % per_tile)
        value = comb[slot, r // per_tile]
        return pltpu.roll(value, LANES - shift, 1) if shift else value

    nothing = jnp.zeros((dirs, LANES), jnp.float32)
    field[0, :, width:] = nothing
    field[rows + 3, :, width:] = nothing
    field[1, :, width:] = edge_tile(0, rows - 1)
    field[rows + 2, :, width:] = edge_tile(2, 0)
    for r in range(rows):
        field[r + 2, :, width:] = edge_tile(1, r)
    for copy in loads[base + 2:]:
        copy.wait()
    for copy in raw_copies:
        copy.wait_recv()
    for r in range(rows):
        for t in range(tiles):
            field[r + 2, :, t * LANES:(t + 1) * LANES] = land[t, pl.ds(r, dirs, stride=rows), :]

    def stencil(coef, before, centre, after):
        def spread(c):
            return jnp.broadcast_to(c, (dirs, c.shape[-1]))
        north = pltpu.roll(centre, wide - 1, 1)
        south = pltpu.roll(centre, 1, 1)
        keep = coef[0].shape[-1]
        return (spread(coef[0]) * after[:, :keep] + spread(coef[1]) * before[:, :keep]
                + spread(coef[2]) * north[:, :keep] + spread(coef[3]) * south[:, :keep]
                + spread(coef[4]) * centre[:, :keep])

    for r in (-1, rows):
        first[r + 1] = stencil([coef0[i, BLOCK + r:BLOCK + r + 1, :] for i in range(5)],
                               field[r + 1], field[r + 2], field[r + 3])

    def first_block(b, _):
        start = pl.multiple_of(b * BLOCK, BLOCK)
        coef = [coef0[i, pl.ds(start + BLOCK, BLOCK), :] for i in range(5)]
        for k in range(BLOCK):
            first[start + k + 1] = stencil([c[k:k + 1] for c in coef], field[start + k + 1],
                                           field[start + k + 2], field[start + k + 3])
        return 0

    lax.fori_loop(0, blocks, first_block, 0)

    stack = BLOCK * dirs

    def second_block(b, total):
        start = pl.multiple_of(b * BLOCK, BLOCK)
        coef = [coef1[i, pl.ds(start, BLOCK), :] for i in range(5)]
        for k in range(BLOCK):
            advanced[b, k * dirs:(k + 1) * dirs, :] = stencil(
                [c[k:k + 1] for c in coef], first[start + k], first[start + k + 1], first[start + k + 2])
        part = advanced[b]
        return total + lax.dot_general(part, part, (((1,), (1,)), ((), ())), precision=HIGHEST,
                                       preferred_element_type=jnp.float32)

    total = lax.fori_loop(0, blocks, second_block, jnp.zeros((stack, stack), jnp.float32))
    si = lax.broadcasted_iota(jnp.int32, (stack, stack), 0)
    sj = lax.broadcasted_iota(jnp.int32, (stack, stack), 1)
    total = jnp.where(si // dirs == sj // dirs, total, 0.0)
    gram = total[:dirs]
    for k in range(1, BLOCK):
        gram = gram + total[k * dirs:(k + 1) * dirs]
    turn = stack // 2
    while turn >= dirs:
        gram = gram + pltpu.roll(gram, turn, 1)
        turn //= 2
    gl = lax.broadcasted_iota(jnp.int32, (dirs // 2, stack), 1) < stack // 2
    packed = jnp.where(gl, gram[:dirs // 2], gram[dirs // 2:])

    peers = groups * spans
    at1 = g * spans + z
    gram1[at1] = packed
    copies = []
    for k in range(1, peers):
        to = up(at1, k, peers)
        copies.append(send(gram1.at[at1], gram1.at[at1], g1_send.at[k], g1_recv.at[k],
                           dev(lax.div(to, spans), x, lax.rem(to, spans))))
    for copy in copies:
        copy.wait_recv()
    summed = gram1[0]
    for k in range(1, peers):
        summed = summed + gram1[k]
    gram2[x] = summed
    copies2 = []
    for k in range(1, ranks):
        copies2.append(send(gram2.at[x], gram2.at[x], g2_send.at[k], g2_recv.at[k],
                            dev(g, up(x, k, ranks), z)))
    for copy in copies2:
        copy.wait_recv()
    summed = gram2[0]
    for k in range(1, ranks):
        summed = summed + gram2[k]
    summed = summed * (1.0 / cells)
    turned = pltpu.roll(summed, stack // 2, 1)
    gram = jnp.concatenate([jnp.where(gl, summed, turned), jnp.where(gl, turned, summed)], axis=0)

    ri = lax.broadcasted_iota(jnp.int32, (dirs, stack), 0)
    rj = lax.broadcasted_iota(jnp.int32, (dirs, stack), 1)
    work = jnp.where(rj < dirs, gram, jnp.where(rj % dirs == ri, 1.0, 0.0))
    pivots = jnp.ones((dirs, stack), jnp.float32)
    for k in range(dirs):
        column = jnp.broadcast_to(work[:, k:k + 1], (dirs, stack))
        pivot = jnp.broadcast_to(column[k:k + 1], (dirs, stack))
        row = jnp.broadcast_to(work[k:k + 1], (dirs, stack))
        pivots = jnp.where(ri == k, pivot, pivots)
        work = jnp.where(ri > k, work - column * (row / pivot), work)
    work = work * (1.0 / jnp.sqrt(pivots))
    factor[...] = jnp.where(rj >= ri, work, 0.0)[:, :dirs]
    inverse = jnp.where(rj < dirs, pltpu.roll(work, dirs, 1), work)
    mixer = jnp.concatenate([jnp.broadcast_to(inverse[d:d + 1], (BLOCK, stack)) for d in range(dirs)], axis=0)
    mixer = jnp.where(si % BLOCK == sj // dirs, mixer, 0.0)

    final = []
    for b in range(blocks):
        value = jnp.dot(mixer, advanced[b], precision=HIGHEST, preferred_element_type=jnp.float32)
        for d in range(dirs):
            result[d, b * BLOCK:(b + 1) * BLOCK, :] = value[d * BLOCK:(d + 1) * BLOCK]
        spot = pl.ds(b * BLOCK, BLOCK)
        there = out.at[:, spot, pl.ds(pl.multiple_of(g * width, LANES), width)]
        for k in range(1, groups):
            p = up(g, k, groups)
            final.append(send(result.at[pl.ds(p * own, own), spot, :], there, fin_send.at[k, b],
                              fin_recv.at[k, b], dev(p, x, z)))
        copy = pltpu.make_async_copy(result.at[pl.ds(g * own, own), spot, :], there, fin_send.at[0, b])
        copy.start()
        final.append(copy)
    for copy in row_copies + raw_copies + copies + copies2:
        copy.wait_send()
    for dx in (-1, 1, 0):
        slot = 1 - dx
        for j in range(groups):
            for side, step in ((0, -1), (1, 1)):
                dg = (j + step) % groups

                def left(j=j, side=side, slot=slot):
                    pltpu.make_async_remote_copy(
                        src_ref=col_send.at[j], dst_ref=col_land.at[slot, side, g],
                        send_sem=cs_send.at[slot, side, j], recv_sem=cs_recv.at[slot, side, g],
                        device_id=other, device_id_type=MESH).wait_send()
                if 0 <= j + step < groups and dx == 0:
                    pl.when(g != dg)(left)
                else:
                    left()
    for copy in final:
        copy.wait()


def on_device(groups, ranks, spans, primal, tangent, diffusion):
    own, rows, columns = tangent.shape
    width = columns // groups
    tiles = width // LANES
    dirs = own * groups
    stack = BLOCK * dirs
    wide = width + LANES
    col_tiles = -(-rows // (LANES // 4))
    peers = groups * spans
    f32 = jnp.float32
    dma = pltpu.SemaphoreType.DMA
    hbm = pl.BlockSpec(memory_space=pl.ANY)
    basis, factor = pl.pallas_call(
        functools.partial(kernel, groups, ranks, spans),
        out_shape=(jax.ShapeDtypeStruct((own, rows, columns), f32), jax.ShapeDtypeStruct((dirs, dirs), f32)),
        in_specs=[hbm, hbm, hbm],
        out_specs=(hbm, pl.BlockSpec(memory_space=pltpu.VMEM)),
        scratch_shapes=[
            pltpu.VMEM((groups * tiles, own * rows, LANES), f32),
            pltpu.VMEM((tiles, dirs * rows, LANES), f32),
            pltpu.VMEM(primal.shape, f32),
            pltpu.VMEM((rows, width), f32),
            pltpu.VMEM((2, groups, 2, own, width), f32),
            pltpu.VMEM((2, groups, 2, own, width), f32),
            pltpu.VMEM((groups, col_tiles, own, LANES), f32),
            pltpu.VMEM((3, 2, groups, col_tiles, own, LANES), f32),
            pltpu.VMEM((3, col_tiles, dirs, LANES), f32),
            pltpu.VMEM((2, rows, LANES), f32),
            pltpu.VMEM((2, rows, LANES), f32),
            pltpu.VMEM((2, 8, width), f32),
            pltpu.VMEM((2, 8, width), f32),
            pltpu.VMEM((rows + 4, dirs, wide), f32),
            pltpu.VMEM((rows + 2, dirs, wide), f32),
            pltpu.VMEM((5, rows + 2 * BLOCK, wide), f32),
            pltpu.VMEM((5, rows, width), f32),
            pltpu.VMEM((rows // BLOCK, stack, width), f32),
            pltpu.VMEM((peers, dirs // 2, stack), f32),
            pltpu.VMEM((ranks, dirs // 2, stack), f32),
            pltpu.VMEM((dirs, rows, width), f32),
            dma((groups * tiles + 2 + tiles,)),
            dma((groups, tiles)), dma((groups, tiles)),
            dma((2, groups)), dma((2, groups)),
            dma((3, 2, groups)), dma((3, 2, groups)),
            dma((2,)), dma((2,)),
            dma((2,)), dma((2,)),
            dma((peers,)), dma((peers,)),
            dma((ranks,)), dma((ranks,)),
            dma((groups, rows // BLOCK)), dma((groups, rows // BLOCK)),
        ],
        compiler_params=pltpu.CompilerParams(collective_id=0, has_side_effects=True),
    )(primal, tangent.reshape(own * rows, columns), diffusion)
    return basis, factor


def solution(mesh):
    sizes = dict(mesh.shape)
    in_specs = (P(None, None, "gx", ("gz", "grp")), P("grp", "gx", "gz"), P("gx", "gz"))
    out_specs = (P("grp", "gx", "gz"), P())
    return jax.shard_map(
        functools.partial(on_device, sizes["grp"], sizes["gx"], sizes["gz"]),
        mesh=mesh, in_specs=in_specs, out_specs=out_specs, check_vma=False)
```

```python
import functools
import jax
import jax.numpy as jnp
from jax import lax
from jax.experimental import pallas as pl
from jax.experimental.pallas import tpu as pltpu
from jax.sharding import PartitionSpec as P

time_step = 0.25
LANES = 128
BLOCK = 8
MESH = pl.DeviceIdType.MESH
HIGHEST = lax.Precision.HIGHEST


def coefficients(velocity, diffusion):
    half_u = 0.5 * velocity[0]
    half_v = 0.5 * velocity[1]
    return (
        time_step * (diffusion - half_u),
        time_step * (diffusion + half_u),
        time_step * (diffusion - half_v),
        time_step * (diffusion + half_v),
        1.0 - time_step * (4.0 * diffusion + velocity[2]),
    )


def kernel(groups, ranks, spans, primal, tangent, diffusion, out, factor,
           mine, land, prim, diff, row_send, row_land, col_send, col_land, comb,
           vcol_send, vcol_land, vrow_send, vrow_land,
           field, first, coef0, coef1, advanced, far, gram1, gram2, result,
           load_sem, raw_send, raw_recv, rs_send, rs_recv, cs_send, cs_recv,
           vc_send, vc_recv, vr_send, vr_recv, g1_send, g1_recv, g2_send, g2_recv,
           fin_send, fin_recv, early_send, early_recv):
    own, rows, columns = out.shape
    width = columns // groups
    tiles = width // LANES
    dirs = own * groups
    blocks = rows // BLOCK
    wide = width + LANES
    cells = rows * columns * ranks * spans
    g, x, z = lax.axis_index("grp"), lax.axis_index("gx"), lax.axis_index("gz")

    def dev(a, b, c):
        return {"grp": a, "gx": b, "gz": c}

    def up(i, k, n):
        return lax.rem(i + k + n, n)

    loads = []
    for t in range(groups * tiles):
        loads.append(pltpu.make_async_copy(
            tangent.at[:, pl.ds(t * LANES, LANES)], mine.at[t], load_sem.at[t]))
    base = groups * tiles
    loads.append(pltpu.make_async_copy(primal, prim, load_sem.at[base]))
    loads.append(pltpu.make_async_copy(
        diffusion.at[:, pl.ds(pl.multiple_of(g * width, LANES), width)], diff, load_sem.at[base + 1]))
    for t in range(tiles):
        loads.append(pltpu.make_async_copy(
            tangent.at[:, pl.ds(pl.multiple_of(g * width + t * LANES, LANES), LANES)],
            land.at[t, pl.ds(pl.multiple_of(g * own * rows, 8), own * rows), :], load_sem.at[base + 2 + t]))
    for copy in loads:
        copy.start()

    if own < dirs:
        far[...] = jnp.zeros_like(far)

    barrier = pltpu.get_barrier_semaphore()
    greeted = set()
    for dg in range(groups):
        for dx in (-1, 0, 1):
            for dz in (-1, 0, 1):
                greeted.add((dg, dx % ranks, dz % spans))
        for dz in range(spans):
            greeted.add((dg, 0, dz))
    for dx in range(ranks):
        greeted.add((0, dx, 0))
    greeted.discard((0, 0, 0))
    for dg, dx, dz in sorted(greeted):
        pl.semaphore_signal(barrier, inc=1, device_id=dev(up(g, dg, groups), up(x, dx, ranks), up(z, dz, spans)),
                            device_id_type=MESH)
    def send(src, dst, s_sem, r_sem, to):
        copy = pltpu.make_async_remote_copy(src_ref=src, dst_ref=dst, send_sem=s_sem, recv_sem=r_sem,
                                            device_id=to, device_id_type=MESH)
        copy.start()
        return copy

    for copy in loads[:base + 2]:
        copy.wait()

    lane = lax.broadcasted_iota(jnp.int32, (own, LANES), 1)
    per_tile = LANES // 4
    col_tiles = -(-rows // per_tile)
    for j in range(groups):
        for c in range(col_tiles):
            acc = jnp.zeros((own, LANES), jnp.float32)
            for r in range(c * per_tile, min(rows, (c + 1) * per_tile)):
                edge = mine[j * tiles, pl.ds(r, own, stride=rows), :]
                if tiles > 1:
                    edge = jnp.where(lane < LANES // 2, edge,
                                     mine[j * tiles + tiles - 1, pl.ds(r, own, stride=rows), :])
                shift = 4 * (r - c * per_tile)
                if shift:
                    edge = pltpu.roll(edge, shift, 1)
                acc = jnp.where(((lane + (LANES + 2 - shift)) % LANES) < 4, edge, acc)
            col_send[j, c] = acc
    for side, picks in ((0, (0, 1)), (1, (rows - 2, rows - 1))):
        for j in range(groups):
            for i, r in enumerate(picks):
                for t in range(tiles):
                    row_send[side, j, i, :, t * LANES:(t + 1) * LANES] = mine[
                        j * tiles + t, pl.ds(r, own, stride=rows), :]
    for side, r in ((0, 0), (1, rows - 1)):
        for f in range(3):
            vrow_send[side, f:f + 1, :] = prim[0, f, r:r + 1, :]
        vrow_send[side, 3:4, :] = diff[r:r + 1, :]
        vrow_send[side, 4:8, :] = jnp.zeros((4, width), jnp.float32)
    vlane = lax.broadcasted_iota(jnp.int32, (rows, LANES), 1)
    left_acc = jnp.zeros((rows, LANES), jnp.float32)
    right_acc = jnp.zeros((rows, LANES), jnp.float32)
    for f in range(4):
        whole_field = prim[0, f] if f < 3 else diff[...]
        left = whole_field[:, :LANES]
        right = whole_field[:, width - LANES:]
        if f:
            left = pltpu.roll(left, f, 1)
            right = pltpu.roll(right, LANES - f, 1)
        left_acc = jnp.where(vlane == f, left, left_acc)
        right_acc = jnp.where(vlane == LANES - 1 - f, right, right_acc)
    vcol_send[0] = left_acc
    vcol_send[1] = right_acc

    for i, value in enumerate(coefficients([prim[1, f] for f in range(3)], diff[...])):
        coef1[i] = value

    pl.semaphore_wait(barrier, len(greeted))

    row_copies = []
    for side, dx in ((0, -1), (1, 1)):
        for k in range(groups):
            p = up(g, k + 1, groups)
            row_copies.append(send(row_send.at[side, p], row_land.at[side, g], rs_send.at[side, k],
                                   rs_recv.at[side, k], dev(p, up(x, dx, ranks), z)))
        row_copies.append(send(vrow_send.at[side], vrow_land.at[side], vr_send.at[side], vr_recv.at[side],
                               dev(g, up(x, dx, ranks), z)))
    chunk = z * groups + g
    chunks = spans * groups
    for side, step in ((0, -1), (1, 1)):
        to = up(chunk, step, chunks)
        row_copies.append(send(vcol_send.at[side], vcol_land.at[side], vc_send.at[side], vc_recv.at[side],
                               dev(lax.rem(to, groups), x, lax.div(to, groups))))
    for dx in (-1, 1, 0):
        slot = 1 - dx
        for j in range(groups):
            for side, step in ((0, -1), (1, 1)):
                dg = (j + step) % groups
                inside = 0 <= j + step < groups
                dz = z if inside else up(z, step, spans)

                def issue(j=j, side=side, dg=dg, dz=dz, slot=slot, dx=dx):
                    send(col_send.at[j], col_land.at[slot, side, g], cs_send.at[slot, side, j],
                         cs_recv.at[slot, side, g], dev(dg, up(x, dx, ranks), dz))
                if inside and dx == 0:
                    pl.when(g != dg)(issue)

                    @pl.when(g == dg)
                    def _(j=j, side=side, dg=dg, slot=slot):
                        col_land[slot, side, dg] = col_send[j]
                else:
                    issue()
    raw_copies = []
    for k in range(1, groups):
        p = up(g, k, groups)
        for t in range(tiles):
            raw_copies.append(send(
                tangent.at[:, pl.ds(pl.multiple_of(p * width + t * LANES, LANES), LANES)],
                land.at[t, pl.ds(pl.multiple_of(g * own * rows, 8), own * rows), :],
                raw_send.at[k, t], raw_recv.at[k, t], dev(p, x, z)))


    for copy in row_copies:
        copy.wait_recv()
    halo = []
    for f in range(4):
        after, before = vcol_land[0], vcol_land[1]
        if f:
            after = pltpu.roll(after, LANES - f, 1)
            before = pltpu.roll(before, f, 1)
        halo.append(jnp.where(vlane < LANES // 2, after, before))
    for i, value in enumerate(coefficients([prim[0, f] for f in range(3)], diff[...])):
        coef0[i, BLOCK:BLOCK + rows, :width] = value
    for i, value in enumerate(coefficients(halo[:3], halo[3])):
        coef0[i, BLOCK:BLOCK + rows, width:] = value
    for side, at in ((0, BLOCK + rows), (1, BLOCK - 1)):
        part = [vrow_land[side, f:f + 1, :] for f in range(4)]
        for i, value in enumerate(coefficients(part[:3], part[3])):
            coef0[i, at:at + 1, :width] = value
            coef0[i, at:at + 1, width:] = jnp.zeros((1, LANES), jnp.float32)

    for side, at in ((0, rows + 2), (1, 0)):
        for s in range(groups):
            for i in range(2):
                field[at + i, s * own:(s + 1) * own, :width] = row_land[side, s, i]

    other = dev(up(g, 1, groups), x, z)
    for slot in range(3):
        for side in range(2):
            for s in range(groups):
                def arrived(slot=slot, side=side, s=s):
                    pltpu.make_async_remote_copy(
                        src_ref=col_send.at[0], dst_ref=col_land.at[slot, side, s],
                        send_sem=cs_send.at[slot, side, 0], recv_sem=cs_recv.at[slot, side, s],
                        device_id=other, device_id_type=MESH).wait_recv()
                if slot == 1:
                    inside = (g < groups - 1) if side == 0 else (g > 0)
                    pl.when(jnp.logical_not(jnp.logical_and(inside, g == s)))(arrived)
                else:
                    arrived()
    for slot in range(3):
        for c in range(col_tiles):
            for s in range(groups):
                comb[slot, c, s * own:(s + 1) * own, :] = jnp.where(
                    lane % 4 < 2, col_land[slot, 0, s, c], col_land[slot, 1, s, c])

    def edge_tile(slot, r):
        shift = 4 * (r % per_tile)
        value = comb[slot, r // per_tile]
        return pltpu.roll(value, LANES - shift, 1) if shift else value

    nothing = jnp.zeros((dirs, LANES), jnp.float32)
    field[0, :, width:] = nothing
    field[rows + 3, :, width:] = nothing
    field[1, :, width:] = edge_tile(0, rows - 1)
    field[rows + 2, :, width:] = edge_tile(2, 0)
    for r in range(rows):
        field[r + 2, :, width:] = edge_tile(1, r)
    for copy in loads[base + 2:]:
        copy.wait()
    for copy in raw_copies:
        copy.wait_recv()
    for r in range(rows):
        for t in range(tiles):
            field[r + 2, :, t * LANES:(t + 1) * LANES] = land[t, pl.ds(r, dirs, stride=rows), :]

    def stencil(coef, before, centre, after):
        def spread(c):
            return jnp.broadcast_to(c, (dirs, c.shape[-1]))
        north = pltpu.roll(centre, wide - 1, 1)
        south = pltpu.roll(centre, 1, 1)
        keep = coef[0].shape[-1]
        return (spread(coef[0]) * after[:, :keep] + spread(coef[1]) * before[:, :keep]
                + spread(coef[2]) * north[:, :keep] + spread(coef[3]) * south[:, :keep]
                + spread(coef[4]) * centre[:, :keep])

    for r in (-1, rows):
        first[r + 1] = stencil([coef0[i, BLOCK + r:BLOCK + r + 1, :] for i in range(5)],
                               field[r + 1], field[r + 2], field[r + 3])

    def first_block(b, _):
        start = pl.multiple_of(b * BLOCK, BLOCK)
        coef = [coef0[i, pl.ds(start + BLOCK, BLOCK), :] for i in range(5)]
        for k in range(BLOCK):
            first[start + k + 1] = stencil([c[k:k + 1] for c in coef], field[start + k + 1],
                                           field[start + k + 2], field[start + k + 3])
        return 0

    lax.fori_loop(0, blocks, first_block, 0)

    stack = BLOCK * dirs

    def second_block(b, total):
        start = pl.multiple_of(b * BLOCK, BLOCK)
        coef = [coef1[i, pl.ds(start, BLOCK), :] for i in range(5)]
        for k in range(BLOCK):
            advanced[start + k] = stencil(
                [c[k:k + 1] for c in coef], first[start + k], first[start + k + 1], first[start + k + 2])
        part = advanced[pl.ds(start, BLOCK)].reshape(stack, width)
        return total + lax.dot_general(part, part, (((1,), (1,)), ((), ())), precision=HIGHEST,
                                       preferred_element_type=jnp.float32)

    total = lax.fori_loop(0, blocks, second_block, jnp.zeros((stack, stack), jnp.float32))
    si = lax.broadcasted_iota(jnp.int32, (stack, stack), 0)
    sj = lax.broadcasted_iota(jnp.int32, (stack, stack), 1)
    total = jnp.where(si // dirs == sj // dirs, total, 0.0)
    gram = total[:dirs]
    for k in range(1, BLOCK):
        gram = gram + total[k * dirs:(k + 1) * dirs]
    turn = stack // 2
    while turn >= dirs:
        gram = gram + pltpu.roll(gram, turn, 1)
        turn //= 2
    gl = lax.broadcasted_iota(jnp.int32, (dirs // 2, stack), 1) < stack // 2
    packed = jnp.where(gl, gram[:dirs // 2], gram[dirs // 2:])

    peers = groups * spans
    at1 = g * spans + z
    gram1[at1] = packed
    copies = []
    for k in range(1, peers):
        to = up(at1, k, peers)
        copies.append(send(gram1.at[at1], gram1.at[at1], g1_send.at[k], g1_recv.at[k],
                           dev(lax.div(to, spans), x, lax.rem(to, spans))))
    need = [min(dirs, -(-(p + 1) * own // BLOCK) * BLOCK) for p in range(groups)]
    soon = [min(blocks, blocks * dirs // (2 * need[p])) for p in range(groups)]

    def early(p, k, b):
        part = (pl.ds(b * BLOCK, BLOCK), pl.ds(0, need[p]), slice(None))
        return pltpu.make_async_remote_copy(
            src_ref=advanced.at[part], dst_ref=far.at[(k - 1, *part)], send_sem=early_send.at[k, b],
            recv_sem=early_recv.at[k, b], device_id=dev(up(g, k, groups), x, z), device_id_type=MESH)

    def late(p, k, b):
        spot = pl.ds(b * BLOCK, BLOCK)
        return pltpu.make_async_remote_copy(
            src_ref=result.at[pl.ds(p * own, own), spot, :],
            dst_ref=out.at[:, spot, pl.ds(pl.multiple_of(g * width, LANES), width)],
            send_sem=fin_send.at[k, b], recv_sem=fin_recv.at[k, b],
            device_id=dev(up(g, k, groups), x, z), device_id_type=MESH)

    def to_peers(act):
        for s in range(groups):
            @pl.when(g == s)
            def _(s=s):
                for k in range(1, groups):
                    act((s + k) % groups, k)

    @to_peers
    def _(p, k):
        for b in range(soon[p]):
            early(p, k, b).start()

    for copy in copies:
        copy.wait_recv()
    summed = gram1[0]
    for k in range(1, peers):
        summed = summed + gram1[k]
    gram2[x] = summed
    copies2 = []
    for k in range(1, ranks):
        copies2.append(send(gram2.at[x], gram2.at[x], g2_send.at[k], g2_recv.at[k],
                            dev(g, up(x, k, ranks), z)))
    for copy in copies2:
        copy.wait_recv()
    summed = gram2[0]
    for k in range(1, ranks):
        summed = summed + gram2[k]
    summed = summed * (1.0 / cells)
    turned = pltpu.roll(summed, stack // 2, 1)
    gram = jnp.concatenate([jnp.where(gl, summed, turned), jnp.where(gl, turned, summed)], axis=0)

    ri = lax.broadcasted_iota(jnp.int32, (dirs, stack), 0)
    rj = lax.broadcasted_iota(jnp.int32, (dirs, stack), 1)
    work = jnp.where(rj < dirs, gram, jnp.where(rj % dirs == ri, 1.0, 0.0))
    pivots = jnp.ones((dirs, stack), jnp.float32)
    for k in range(dirs):
        column = jnp.broadcast_to(work[:, k:k + 1], (dirs, stack))
        pivot = jnp.broadcast_to(column[k:k + 1], (dirs, stack))
        row = jnp.broadcast_to(work[k:k + 1], (dirs, stack))
        pivots = jnp.where(ri == k, pivot, pivots)
        work = jnp.where(ri > k, work - column * (row / pivot), work)
    work = work * (1.0 / jnp.sqrt(pivots))
    factor[...] = jnp.where(rj >= ri, work, 0.0)[:, :dirs]
    inverse = jnp.where(rj < dirs, pltpu.roll(work, dirs, 1), work)
    mixer = jnp.concatenate([jnp.broadcast_to(inverse[d:d + 1], (BLOCK, stack)) for d in range(dirs)], axis=0)
    mixer = jnp.where(si % BLOCK == sj // dirs, mixer, 0.0)

    def mixed(p, block):
        return jnp.dot(mixer[p * own * BLOCK:(p + 1) * own * BLOCK], block.reshape(stack, width),
                       precision=HIGHEST, preferred_element_type=jnp.float32)

    @to_peers
    def _(p, k):
        for b in range(soon[p], blocks):
            value = mixed(p, advanced[b * BLOCK:(b + 1) * BLOCK])
            for d in range(own):
                result[p * own + d, b * BLOCK:(b + 1) * BLOCK, :] = value[d * BLOCK:(d + 1) * BLOCK]
            late(p, k, b).start()

    for p in range(groups):
        @pl.when(g == p)
        def _(p=p):
            def put(value, b, s):
                for d in range(own):
                    out[d, b * BLOCK:(b + 1) * BLOCK, s * width:(s + 1) * width] = value[d * BLOCK:(d + 1) * BLOCK]

            for b in range(blocks):
                put(mixed(p, advanced[b * BLOCK:(b + 1) * BLOCK]), b, p)
            for b in range(soon[p]):
                for k in range(1, groups):
                    early(p, k, b).wait_recv()
                    put(mixed(p, far[k - 1, b * BLOCK:(b + 1) * BLOCK]), b, (p - k) % groups)
            for b in range(soon[p], blocks):
                for k in range(1, groups):
                    late(p, k, b).wait_recv()

    @to_peers
    def _(p, k):
        for b in range(soon[p]):
            early(p, k, b).wait_send()
        for b in range(soon[p], blocks):
            late(p, k, b).wait_send()

    for copy in row_copies + raw_copies + copies + copies2:
        copy.wait_send()
    for dx in (-1, 1, 0):
        slot = 1 - dx
        for j in range(groups):
            for side, step in ((0, -1), (1, 1)):
                dg = (j + step) % groups

                def left(j=j, side=side, slot=slot):
                    pltpu.make_async_remote_copy(
                        src_ref=col_send.at[j], dst_ref=col_land.at[slot, side, g],
                        send_sem=cs_send.at[slot, side, j], recv_sem=cs_recv.at[slot, side, g],
                        device_id=other, device_id_type=MESH).wait_send()
                if 0 <= j + step < groups and dx == 0:
                    pl.when(g != dg)(left)
                else:
                    left()


def write_out(basis, factor, basis_out, factor_out, sem):
    copies = [pltpu.make_async_copy(basis, basis_out, sem.at[0]),
              pltpu.make_async_copy(factor, factor_out, sem.at[1])]
    for copy in copies:
        copy.start()
    for copy in copies:
        copy.wait()


def on_device(groups, ranks, spans, primal, tangent, diffusion):
    own, rows, columns = tangent.shape
    width = columns // groups
    tiles = width // LANES
    dirs = own * groups
    stack = BLOCK * dirs
    wide = width + LANES
    col_tiles = -(-rows // (LANES // 4))
    peers = groups * spans
    f32 = jnp.float32
    dma = pltpu.SemaphoreType.DMA
    hbm = pl.BlockSpec(memory_space=pl.ANY)
    vmem = pl.BlockSpec(memory_space=pltpu.VMEM)
    basis, factor = pl.pallas_call(
        functools.partial(kernel, groups, ranks, spans),
        out_shape=(pltpu.VMEM((own, rows, columns), f32), pltpu.VMEM((dirs, dirs), f32)),
        in_specs=[hbm, hbm, hbm],
        out_specs=(vmem, vmem),
        scratch_shapes=[
            pltpu.VMEM((groups * tiles, own * rows, LANES), f32),
            pltpu.VMEM((tiles, dirs * rows, LANES), f32),
            pltpu.VMEM(primal.shape, f32),
            pltpu.VMEM((rows, width), f32),
            pltpu.VMEM((2, groups, 2, own, width), f32),
            pltpu.VMEM((2, groups, 2, own, width), f32),
            pltpu.VMEM((groups, col_tiles, own, LANES), f32),
            pltpu.VMEM((3, 2, groups, col_tiles, own, LANES), f32),
            pltpu.VMEM((3, col_tiles, dirs, LANES), f32),
            pltpu.VMEM((2, rows, LANES), f32),
            pltpu.VMEM((2, rows, LANES), f32),
            pltpu.VMEM((2, 8, width), f32),
            pltpu.VMEM((2, 8, width), f32),
            pltpu.VMEM((rows + 4, dirs, wide), f32),
            pltpu.VMEM((rows + 2, dirs, wide), f32),
            pltpu.VMEM((5, rows + 2 * BLOCK, wide), f32),
            pltpu.VMEM((5, rows, width), f32),
            pltpu.VMEM((rows, dirs, width), f32),
            pltpu.VMEM((groups - 1, rows, dirs, width), f32),
            pltpu.VMEM((peers, dirs // 2, stack), f32),
            pltpu.VMEM((ranks, dirs // 2, stack), f32),
            pltpu.VMEM((dirs, rows, width), f32),
            dma((groups * tiles + 2 + tiles,)),
            dma((groups, tiles)), dma((groups, tiles)),
            dma((2, groups)), dma((2, groups)),
            dma((3, 2, groups)), dma((3, 2, groups)),
            dma((2,)), dma((2,)),
            dma((2,)), dma((2,)),
            dma((peers,)), dma((peers,)),
            dma((ranks,)), dma((ranks,)),
            dma((groups, rows // BLOCK)), dma((groups, rows // BLOCK)),
            dma((groups, rows // BLOCK)), dma((groups, rows // BLOCK)),
        ],
        compiler_params=pltpu.CompilerParams(collective_id=0, has_side_effects=True),
    )(primal, tangent.reshape(own * rows, columns), diffusion)
    return pl.pallas_call(
        write_out,
        out_shape=(jax.ShapeDtypeStruct(basis.shape, f32), jax.ShapeDtypeStruct(factor.shape, f32)),
        in_specs=[vmem, vmem],
        out_specs=(hbm, hbm),
        scratch_shapes=[dma((2,))],
    )(pltpu.with_memory_space_constraint(basis, pltpu.VMEM), pltpu.with_memory_space_constraint(factor, pltpu.VMEM))


def solution(mesh):
    sizes = dict(mesh.shape)
    in_specs = (P(None, None, "gx", ("gz", "grp")), P("grp", "gx", "gz"), P("gx", "gz"))
    out_specs = (P("grp", "gx", "gz"), P())
    return jax.shard_map(
        functools.partial(on_device, sizes["grp"], sizes["gx"], sizes["gz"]),
        mesh=mesh, in_specs=in_specs, out_specs=out_specs, check_vma=False)
```

```python
import functools
import jax
import jax.numpy as jnp
from jax import lax
from jax.experimental import pallas as pl
from jax.experimental.pallas import tpu as pltpu
from jax.sharding import PartitionSpec as P

time_step = 0.25
LANES = 128
BLOCK = 8
MESH = pl.DeviceIdType.MESH
HIGHEST = lax.Precision.HIGHEST


def coefficients(velocity, diffusion):
    half_u = 0.5 * velocity[0]
    half_v = 0.5 * velocity[1]
    return (
        time_step * (diffusion - half_u),
        time_step * (diffusion + half_u),
        time_step * (diffusion - half_v),
        time_step * (diffusion + half_v),
        1.0 - time_step * (4.0 * diffusion + velocity[2]),
    )


def kernel(groups, ranks, spans, primal, tangent, diffusion, out, factor,
           mine, land, prim, diff, row_send, row_land, col_send, col_land, comb,
           vcol_send, vcol_land, vrow_send, vrow_land,
           field, first, coef0, coef1, advanced, far, gram1, gram2, result,
           load_sem, raw_send, raw_recv, rs_send, rs_recv, cs_send, cs_recv,
           vc_send, vc_recv, vr_send, vr_recv, g1_send, g1_recv, g2_send, g2_recv,
           fin_send, fin_recv, early_send, early_recv):
    own, rows, columns = out.shape
    width = columns // groups
    tiles = width // LANES
    dirs = own * groups
    blocks = rows // BLOCK
    wide = width + LANES
    cells = rows * columns * ranks * spans
    g, x, z = lax.axis_index("grp"), lax.axis_index("gx"), lax.axis_index("gz")

    def dev(a, b, c):
        return {"grp": a, "gx": b, "gz": c}

    def up(i, k, n):
        return lax.rem(i + k + n, n)

    loads = []
    for t in range(groups * tiles):
        loads.append(pltpu.make_async_copy(
            tangent.at[:, pl.ds(t * LANES, LANES)], mine.at[t], load_sem.at[t]))
    base = groups * tiles
    loads.append(pltpu.make_async_copy(primal, prim, load_sem.at[base]))
    loads.append(pltpu.make_async_copy(
        diffusion.at[:, pl.ds(pl.multiple_of(g * width, LANES), width)], diff, load_sem.at[base + 1]))
    for t in range(tiles):
        loads.append(pltpu.make_async_copy(
            tangent.at[:, pl.ds(pl.multiple_of(g * width + t * LANES, LANES), LANES)],
            land.at[t, pl.ds(pl.multiple_of(g * own * rows, 8), own * rows), :], load_sem.at[base + 2 + t]))
    for copy in loads:
        copy.start()

    if own < dirs:
        far[...] = jnp.zeros_like(far)

    barrier = pltpu.get_barrier_semaphore()
    greeted = set()
    for dg in range(groups):
        for dx in (-1, 0, 1):
            for dz in (-1, 0, 1):
                greeted.add((dg, dx % ranks, dz % spans))
        for dz in range(spans):
            greeted.add((dg, 0, dz))
    for dx in range(ranks):
        greeted.add((0, dx, 0))
    greeted.discard((0, 0, 0))
    for dg, dx, dz in sorted(greeted):
        pl.semaphore_signal(barrier, inc=1, device_id=dev(up(g, dg, groups), up(x, dx, ranks), up(z, dz, spans)),
                            device_id_type=MESH)
    def send(src, dst, s_sem, r_sem, to):
        copy = pltpu.make_async_remote_copy(src_ref=src, dst_ref=dst, send_sem=s_sem, recv_sem=r_sem,
                                            device_id=to, device_id_type=MESH)
        copy.start()
        return copy

    for copy in loads[:base + 2]:
        copy.wait()

    lane = lax.broadcasted_iota(jnp.int32, (own, LANES), 1)
    per_tile = LANES // 4
    col_tiles = -(-rows // per_tile)
    for j in range(groups):
        for c in range(col_tiles):
            acc = jnp.zeros((own, LANES), jnp.float32)
            for r in range(c * per_tile, min(rows, (c + 1) * per_tile)):
                edge = mine[j * tiles, pl.ds(r, own, stride=rows), :]
                if tiles > 1:
                    edge = jnp.where(lane < LANES // 2, edge,
                                     mine[j * tiles + tiles - 1, pl.ds(r, own, stride=rows), :])
                shift = 4 * (r - c * per_tile)
                if shift:
                    edge = pltpu.roll(edge, shift, 1)
                acc = jnp.where(((lane + (LANES + 2 - shift)) % LANES) < 4, edge, acc)
            col_send[j, c] = acc
    for side, picks in ((0, (0, 1)), (1, (rows - 2, rows - 1))):
        for j in range(groups):
            for i, r in enumerate(picks):
                for t in range(tiles):
                    row_send[side, j, i, :, t * LANES:(t + 1) * LANES] = mine[
                        j * tiles + t, pl.ds(r, own, stride=rows), :]
    for side, r in ((0, 0), (1, rows - 1)):
        for f in range(3):
            vrow_send[side, f:f + 1, :] = prim[0, f, r:r + 1, :]
        vrow_send[side, 3:4, :] = diff[r:r + 1, :]
        vrow_send[side, 4:8, :] = jnp.zeros((4, width), jnp.float32)
    vlane = lax.broadcasted_iota(jnp.int32, (rows, LANES), 1)
    left_acc = jnp.zeros((rows, LANES), jnp.float32)
    right_acc = jnp.zeros((rows, LANES), jnp.float32)
    for f in range(4):
        whole_field = prim[0, f] if f < 3 else diff[...]
        left = whole_field[:, :LANES]
        right = whole_field[:, width - LANES:]
        if f:
            left = pltpu.roll(left, f, 1)
            right = pltpu.roll(right, LANES - f, 1)
        left_acc = jnp.where(vlane == f, left, left_acc)
        right_acc = jnp.where(vlane == LANES - 1 - f, right, right_acc)
    vcol_send[0] = left_acc
    vcol_send[1] = right_acc

    for i, value in enumerate(coefficients([prim[1, f] for f in range(3)], diff[...])):
        coef1[i] = value

    pl.semaphore_wait(barrier, len(greeted))

    row_copies = []
    for side, dx in ((0, -1), (1, 1)):
        for k in range(groups):
            p = up(g, k + 1, groups)
            row_copies.append(send(row_send.at[side, p], row_land.at[side, g], rs_send.at[side, k],
                                   rs_recv.at[side, k], dev(p, up(x, dx, ranks), z)))
        row_copies.append(send(vrow_send.at[side], vrow_land.at[side], vr_send.at[side], vr_recv.at[side],
                               dev(g, up(x, dx, ranks), z)))
    chunk = z * groups + g
    chunks = spans * groups
    for side, step in ((0, -1), (1, 1)):
        to = up(chunk, step, chunks)
        row_copies.append(send(vcol_send.at[side], vcol_land.at[side], vc_send.at[side], vc_recv.at[side],
                               dev(lax.rem(to, groups), x, lax.div(to, groups))))
    for dx in (-1, 1, 0):
        slot = 1 - dx
        for j in range(groups):
            for side, step in ((0, -1), (1, 1)):
                dg = (j + step) % groups
                inside = 0 <= j + step < groups
                dz = z if inside else up(z, step, spans)

                def issue(j=j, side=side, dg=dg, dz=dz, slot=slot, dx=dx):
                    send(col_send.at[j], col_land.at[slot, side, g], cs_send.at[slot, side, j],
                         cs_recv.at[slot, side, g], dev(dg, up(x, dx, ranks), dz))
                if inside and dx == 0:
                    pl.when(g != dg)(issue)

                    @pl.when(g == dg)
                    def _(j=j, side=side, dg=dg, slot=slot):
                        col_land[slot, side, dg] = col_send[j]
                else:
                    issue()
    raw_copies = []
    for k in range(1, groups):
        p = up(g, k, groups)
        for t in range(tiles):
            raw_copies.append(send(
                tangent.at[:, pl.ds(pl.multiple_of(p * width + t * LANES, LANES), LANES)],
                land.at[t, pl.ds(pl.multiple_of(g * own * rows, 8), own * rows), :],
                raw_send.at[k, t], raw_recv.at[k, t], dev(p, x, z)))


    for copy in row_copies:
        copy.wait_recv()
    halo = []
    for f in range(4):
        after, before = vcol_land[0], vcol_land[1]
        if f:
            after = pltpu.roll(after, LANES - f, 1)
            before = pltpu.roll(before, f, 1)
        halo.append(jnp.where(vlane < LANES // 2, after, before))
    for i, value in enumerate(coefficients([prim[0, f] for f in range(3)], diff[...])):
        coef0[i, BLOCK:BLOCK + rows, :width] = value
    for i, value in enumerate(coefficients(halo[:3], halo[3])):
        coef0[i, BLOCK:BLOCK + rows, width:] = value
    for side, at in ((0, BLOCK + rows), (1, BLOCK - 1)):
        part = [vrow_land[side, f:f + 1, :] for f in range(4)]
        for i, value in enumerate(coefficients(part[:3], part[3])):
            coef0[i, at:at + 1, :width] = value
            coef0[i, at:at + 1, width:] = jnp.zeros((1, LANES), jnp.float32)

    for side, at in ((0, rows + 2), (1, 0)):
        for s in range(groups):
            for i in range(2):
                field[at + i, s * own:(s + 1) * own, :width] = row_land[side, s, i]

    other = dev(up(g, 1, groups), x, z)
    for slot in range(3):
        for side in range(2):
            for s in range(groups):
                def arrived(slot=slot, side=side, s=s):
                    pltpu.make_async_remote_copy(
                        src_ref=col_send.at[0], dst_ref=col_land.at[slot, side, s],
                        send_sem=cs_send.at[slot, side, 0], recv_sem=cs_recv.at[slot, side, s],
                        device_id=other, device_id_type=MESH).wait_recv()
                if slot == 1:
                    inside = (g < groups - 1) if side == 0 else (g > 0)
                    pl.when(jnp.logical_not(jnp.logical_and(inside, g == s)))(arrived)
                else:
                    arrived()
    for slot in range(3):
        for c in range(col_tiles):
            for s in range(groups):
                comb[slot, c, s * own:(s + 1) * own, :] = jnp.where(
                    lane % 4 < 2, col_land[slot, 0, s, c], col_land[slot, 1, s, c])

    def edge_tile(slot, r):
        shift = 4 * (r % per_tile)
        value = comb[slot, r // per_tile]
        return pltpu.roll(value, LANES - shift, 1) if shift else value

    nothing = jnp.zeros((dirs, LANES), jnp.float32)
    field[0, :, width:] = nothing
    field[rows + 3, :, width:] = nothing
    field[1, :, width:] = edge_tile(0, rows - 1)
    field[rows + 2, :, width:] = edge_tile(2, 0)
    for r in range(rows):
        field[r + 2, :, width:] = edge_tile(1, r)
    for copy in loads[base + 2:]:
        copy.wait()
    for copy in raw_copies:
        copy.wait_recv()
    for r in range(rows):
        for t in range(tiles):
            field[r + 2, :, t * LANES:(t + 1) * LANES] = land[t, pl.ds(r, dirs, stride=rows), :]

    def stencil(coef, before, centre, after):
        def spread(c):
            return jnp.broadcast_to(c, (dirs, c.shape[-1]))
        north = pltpu.roll(centre, wide - 1, 1)
        south = pltpu.roll(centre, 1, 1)
        keep = coef[0].shape[-1]
        return (spread(coef[0]) * after[:, :keep] + spread(coef[1]) * before[:, :keep]
                + spread(coef[2]) * north[:, :keep] + spread(coef[3]) * south[:, :keep]
                + spread(coef[4]) * centre[:, :keep])

    for r in (-1, rows):
        first[r + 1] = stencil([coef0[i, BLOCK + r:BLOCK + r + 1, :] for i in range(5)],
                               field[r + 1], field[r + 2], field[r + 3])

    def first_block(b, _):
        start = pl.multiple_of(b * BLOCK, BLOCK)
        coef = [coef0[i, pl.ds(start + BLOCK, BLOCK), :] for i in range(5)]
        for k in range(BLOCK):
            first[start + k + 1] = stencil([c[k:k + 1] for c in coef], field[start + k + 1],
                                           field[start + k + 2], field[start + k + 3])
        return 0

    lax.fori_loop(0, blocks, first_block, 0)

    stack = BLOCK * dirs

    def second_block(b, total):
        start = pl.multiple_of(b * BLOCK, BLOCK)
        coef = [coef1[i, pl.ds(start, BLOCK), :] for i in range(5)]
        for k in range(BLOCK):
            advanced[start + k] = stencil(
                [c[k:k + 1] for c in coef], first[start + k], first[start + k + 1], first[start + k + 2])
        part = advanced[pl.ds(start, BLOCK)].reshape(stack, width)
        return total + lax.dot_general(part, part, (((1,), (1,)), ((), ())), precision=HIGHEST,
                                       preferred_element_type=jnp.float32)

    total = lax.fori_loop(0, blocks, second_block, jnp.zeros((stack, stack), jnp.float32))
    si = lax.broadcasted_iota(jnp.int32, (stack, stack), 0)
    sj = lax.broadcasted_iota(jnp.int32, (stack, stack), 1)
    total = jnp.where(si // dirs == sj // dirs, total, 0.0)
    gram = total[:dirs]
    for k in range(1, BLOCK):
        gram = gram + total[k * dirs:(k + 1) * dirs]
    turn = stack // 2
    while turn >= dirs:
        gram = gram + pltpu.roll(gram, turn, 1)
        turn //= 2
    gl = lax.broadcasted_iota(jnp.int32, (dirs // 2, stack), 1) < stack // 2
    packed = jnp.where(gl, gram[:dirs // 2], gram[dirs // 2:])

    peers = groups * spans
    at1 = g * spans + z
    gram1[at1] = packed
    copies = []
    for k in range(1, peers):
        to = up(at1, k, peers)
        copies.append(send(gram1.at[at1], gram1.at[at1], g1_send.at[k], g1_recv.at[k],
                           dev(lax.div(to, spans), x, lax.rem(to, spans))))
    need = [min(dirs, -(-(p + 1) * own // BLOCK) * BLOCK) for p in range(groups)]
    soon = [min(blocks, blocks * dirs // (2 * need[p])) for p in range(groups)]

    def early(p, k, b):
        part = (pl.ds(b * BLOCK, BLOCK), pl.ds(0, need[p]), slice(None))
        return pltpu.make_async_remote_copy(
            src_ref=advanced.at[part], dst_ref=far.at[(k - 1, *part)], send_sem=early_send.at[k, b],
            recv_sem=early_recv.at[k, b], device_id=dev(up(g, k, groups), x, z), device_id_type=MESH)

    def late(p, k, b):
        spot = pl.ds(b * BLOCK, BLOCK)
        return pltpu.make_async_remote_copy(
            src_ref=result.at[pl.ds(p * own, own), spot, :],
            dst_ref=out.at[:, spot, pl.ds(pl.multiple_of(g * width, LANES), width)],
            send_sem=fin_send.at[k, b], recv_sem=fin_recv.at[k, b],
            device_id=dev(up(g, k, groups), x, z), device_id_type=MESH)

    def to_peers(act):
        for s in range(groups):
            @pl.when(g == s)
            def _(s=s):
                for k in range(1, groups):
                    act((s + k) % groups, k)

    @to_peers
    def _(p, k):
        for b in range(soon[p]):
            early(p, k, b).start()

    for copy in copies:
        copy.wait_recv()
    summed = gram1[0]
    for k in range(1, peers):
        summed = summed + gram1[k]
    gram2[x] = summed
    copies2 = []
    for k in range(1, ranks):
        copies2.append(send(gram2.at[x], gram2.at[x], g2_send.at[k], g2_recv.at[k],
                            dev(g, up(x, k, ranks), z)))
    for copy in copies2:
        copy.wait_recv()
    summed = gram2[0]
    for k in range(1, ranks):
        summed = summed + gram2[k]
    summed = summed * (1.0 / cells)
    turned = pltpu.roll(summed, stack // 2, 1)
    gram = jnp.concatenate([jnp.where(gl, summed, turned), jnp.where(gl, turned, summed)], axis=0)

    ri = lax.broadcasted_iota(jnp.int32, (dirs, stack), 0)
    rj = lax.broadcasted_iota(jnp.int32, (dirs, stack), 1)
    work = jnp.where(rj < dirs, gram, jnp.where(rj % dirs == ri, 1.0, 0.0))
    pivots = jnp.ones((dirs, stack), jnp.float32)
    spread_columns = [jnp.broadcast_to(work[:, k:k + 1], (dirs, stack)) for k in range(dirs)]
    for k in range(dirs):
        column = spread_columns[k]
        pivot = jnp.broadcast_to(column[k:k + 1], (dirs, stack))
        scaled = column * (1.0 / pivot)
        for j in range(k + 1, dirs):
            spread_columns[j] = spread_columns[j] - scaled * jnp.broadcast_to(column[j:j + 1], (dirs, stack))
        row = jnp.broadcast_to(work[k:k + 1], (dirs, stack))
        pivots = jnp.where(ri == k, pivot, pivots)
        work = jnp.where(ri > k, work - scaled * row, work)
    work = work * (1.0 / jnp.sqrt(pivots))
    factor[...] = jnp.where(rj >= ri, work, 0.0)[:, :dirs]
    inverse = jnp.where(rj < dirs, pltpu.roll(work, dirs, 1), work)
    mixer = jnp.concatenate([jnp.broadcast_to(inverse[d:d + 1], (BLOCK, stack)) for d in range(dirs)], axis=0)
    mixer = jnp.where(si % BLOCK == sj // dirs, mixer, 0.0)

    def mixed(p, block):
        return jnp.dot(mixer[p * own * BLOCK:(p + 1) * own * BLOCK], block.reshape(stack, width),
                       precision=HIGHEST, preferred_element_type=jnp.float32)

    @to_peers
    def _(p, k):
        for b in range(soon[p], blocks):
            value = mixed(p, advanced[b * BLOCK:(b + 1) * BLOCK])
            for d in range(own):
                result[p * own + d, b * BLOCK:(b + 1) * BLOCK, :] = value[d * BLOCK:(d + 1) * BLOCK]
            late(p, k, b).start()

    for p in range(groups):
        @pl.when(g == p)
        def _(p=p):
            def put(value, b, s):
                for d in range(own):
                    out[d, b * BLOCK:(b + 1) * BLOCK, s * width:(s + 1) * width] = value[d * BLOCK:(d + 1) * BLOCK]

            for b in range(blocks):
                put(mixed(p, advanced[b * BLOCK:(b + 1) * BLOCK]), b, p)
            for b in range(soon[p]):
                for k in range(1, groups):
                    early(p, k, b).wait_recv()
                    put(mixed(p, far[k - 1, b * BLOCK:(b + 1) * BLOCK]), b, (p - k) % groups)
            for b in range(soon[p], blocks):
                for k in range(1, groups):
                    late(p, k, b).wait_recv()

    @to_peers
    def _(p, k):
        for b in range(soon[p]):
            early(p, k, b).wait_send()
        for b in range(soon[p], blocks):
            late(p, k, b).wait_send()

    for copy in row_copies + raw_copies + copies + copies2:
        copy.wait_send()
    for dx in (-1, 1, 0):
        slot = 1 - dx
        for j in range(groups):
            for side, step in ((0, -1), (1, 1)):
                dg = (j + step) % groups

                def left(j=j, side=side, slot=slot):
                    pltpu.make_async_remote_copy(
                        src_ref=col_send.at[j], dst_ref=col_land.at[slot, side, g],
                        send_sem=cs_send.at[slot, side, j], recv_sem=cs_recv.at[slot, side, g],
                        device_id=other, device_id_type=MESH).wait_send()
                if 0 <= j + step < groups and dx == 0:
                    pl.when(g != dg)(left)
                else:
                    left()


def write_out(basis, factor, basis_out, factor_out, sem):
    copies = [pltpu.make_async_copy(basis, basis_out, sem.at[0]),
              pltpu.make_async_copy(factor, factor_out, sem.at[1])]
    for copy in copies:
        copy.start()
    for copy in copies:
        copy.wait()


def on_device(groups, ranks, spans, primal, tangent, diffusion):
    own, rows, columns = tangent.shape
    width = columns // groups
    tiles = width // LANES
    dirs = own * groups
    stack = BLOCK * dirs
    wide = width + LANES
    col_tiles = -(-rows // (LANES // 4))
    peers = groups * spans
    f32 = jnp.float32
    dma = pltpu.SemaphoreType.DMA
    hbm = pl.BlockSpec(memory_space=pl.ANY)
    vmem = pl.BlockSpec(memory_space=pltpu.VMEM)
    basis, factor = pl.pallas_call(
        functools.partial(kernel, groups, ranks, spans),
        out_shape=(pltpu.VMEM((own, rows, columns), f32), pltpu.VMEM((dirs, dirs), f32)),
        in_specs=[hbm, hbm, hbm],
        out_specs=(vmem, vmem),
        scratch_shapes=[
            pltpu.VMEM((groups * tiles, own * rows, LANES), f32),
            pltpu.VMEM((tiles, dirs * rows, LANES), f32),
            pltpu.VMEM(primal.shape, f32),
            pltpu.VMEM((rows, width), f32),
            pltpu.VMEM((2, groups, 2, own, width), f32),
            pltpu.VMEM((2, groups, 2, own, width), f32),
            pltpu.VMEM((groups, col_tiles, own, LANES), f32),
            pltpu.VMEM((3, 2, groups, col_tiles, own, LANES), f32),
            pltpu.VMEM((3, col_tiles, dirs, LANES), f32),
            pltpu.VMEM((2, rows, LANES), f32),
            pltpu.VMEM((2, rows, LANES), f32),
            pltpu.VMEM((2, 8, width), f32),
            pltpu.VMEM((2, 8, width), f32),
            pltpu.VMEM((rows + 4, dirs, wide), f32),
            pltpu.VMEM((rows + 2, dirs, wide), f32),
            pltpu.VMEM((5, rows + 2 * BLOCK, wide), f32),
            pltpu.VMEM((5, rows, width), f32),
            pltpu.VMEM((rows, dirs, width), f32),
            pltpu.VMEM((groups - 1, rows, dirs, width), f32),
            pltpu.VMEM((peers, dirs // 2, stack), f32),
            pltpu.VMEM((ranks, dirs // 2, stack), f32),
            pltpu.VMEM((dirs, rows, width), f32),
            dma((groups * tiles + 2 + tiles,)),
            dma((groups, tiles)), dma((groups, tiles)),
            dma((2, groups)), dma((2, groups)),
            dma((3, 2, groups)), dma((3, 2, groups)),
            dma((2,)), dma((2,)),
            dma((2,)), dma((2,)),
            dma((peers,)), dma((peers,)),
            dma((ranks,)), dma((ranks,)),
            dma((groups, rows // BLOCK)), dma((groups, rows // BLOCK)),
            dma((groups, rows // BLOCK)), dma((groups, rows // BLOCK)),
        ],
        compiler_params=pltpu.CompilerParams(collective_id=0, has_side_effects=True),
    )(primal, tangent.reshape(own * rows, columns), diffusion)
    return pl.pallas_call(
        write_out,
        out_shape=(jax.ShapeDtypeStruct(basis.shape, f32), jax.ShapeDtypeStruct(factor.shape, f32)),
        in_specs=[vmem, vmem],
        out_specs=(hbm, hbm),
        scratch_shapes=[dma((2,))],
    )(pltpu.with_memory_space_constraint(basis, pltpu.VMEM), pltpu.with_memory_space_constraint(factor, pltpu.VMEM))


def solution(mesh):
    sizes = dict(mesh.shape)
    in_specs = (P(None, None, "gx", ("gz", "grp")), P("grp", "gx", "gz"), P("gx", "gz"))
    out_specs = (P("grp", "gx", "gz"), P())
    return jax.shard_map(
        functools.partial(on_device, sizes["grp"], sizes["gx"], sizes["gz"]),
        mesh=mesh, in_specs=in_specs, out_specs=out_specs, check_vma=False)
```

```python
import functools
import jax
import jax.numpy as jnp
from jax import lax
from jax.experimental import pallas as pl
from jax.experimental.pallas import tpu as pltpu
from jax.sharding import PartitionSpec as P

time_step = 0.25
LANES = 128
BLOCK = 8
MESH = pl.DeviceIdType.MESH
HIGHEST = lax.Precision.HIGHEST


def coefficients(velocity, diffusion):
    half_u = 0.5 * velocity[0]
    half_v = 0.5 * velocity[1]
    return (
        time_step * (diffusion - half_u),
        time_step * (diffusion + half_u),
        time_step * (diffusion - half_v),
        time_step * (diffusion + half_v),
        1.0 - time_step * (4.0 * diffusion + velocity[2]),
    )


def kernel(groups, ranks, spans, primal, tangent, diffusion, out, factor,
           mine, land, prim, diff, row_send, row_land, col_send, col_land, comb,
           vcol_send, vcol_land, vrow_send, vrow_land,
           field, first, coef0, coef1, advanced, far, gram1, gram2, result,
           load_sem, raw_send, raw_recv, rs_send, rs_recv, cs_send, cs_recv,
           vc_send, vc_recv, vr_send, vr_recv, g1_send, g1_recv, g2_send, g2_recv,
           fin_send, fin_recv, early_send, early_recv):
    own, rows, columns = out.shape
    width = columns // groups
    tiles = width // LANES
    dirs = own * groups
    blocks = rows // BLOCK
    wide = width + LANES
    cells = rows * columns * ranks * spans
    g, x, z = lax.axis_index("grp"), lax.axis_index("gx"), lax.axis_index("gz")

    def dev(a, b, c):
        return {"grp": a, "gx": b, "gz": c}

    def up(i, k, n):
        return lax.rem(i + k + n, n)

    loads = []
    for t in range(groups * tiles):
        loads.append(pltpu.make_async_copy(
            tangent.at[:, pl.ds(t * LANES, LANES)], mine.at[t], load_sem.at[t]))
    base = groups * tiles
    loads.append(pltpu.make_async_copy(primal, prim, load_sem.at[base]))
    loads.append(pltpu.make_async_copy(
        diffusion.at[:, pl.ds(pl.multiple_of(g * width, LANES), width)], diff, load_sem.at[base + 1]))
    for t in range(tiles):
        loads.append(pltpu.make_async_copy(
            tangent.at[:, pl.ds(pl.multiple_of(g * width + t * LANES, LANES), LANES)],
            land.at[t, pl.ds(pl.multiple_of(g * own * rows, 8), own * rows), :], load_sem.at[base + 2 + t]))
    for copy in loads:
        copy.start()

    if own < dirs:
        far[...] = jnp.zeros_like(far)

    barrier = pltpu.get_barrier_semaphore()
    greeted = set()
    for dg in range(groups):
        for dx in (-1, 0, 1):
            for dz in (-1, 0, 1):
                greeted.add((dg, dx % ranks, dz % spans))
        for dz in range(spans):
            greeted.add((dg, 0, dz))
    for dx in range(ranks):
        greeted.add((0, dx, 0))
    greeted.discard((0, 0, 0))
    for dg, dx, dz in sorted(greeted):
        pl.semaphore_signal(barrier, inc=1, device_id=dev(up(g, dg, groups), up(x, dx, ranks), up(z, dz, spans)),
                            device_id_type=MESH)
    def send(src, dst, s_sem, r_sem, to):
        copy = pltpu.make_async_remote_copy(src_ref=src, dst_ref=dst, send_sem=s_sem, recv_sem=r_sem,
                                            device_id=to, device_id_type=MESH)
        copy.start()
        return copy

    for copy in loads[:base + 2]:
        copy.wait()

    lane = lax.broadcasted_iota(jnp.int32, (own, LANES), 1)
    per_tile = LANES // 4
    col_tiles = -(-rows // per_tile)
    for j in range(groups):
        for c in range(col_tiles):
            acc = jnp.zeros((own, LANES), jnp.float32)
            for r in range(c * per_tile, min(rows, (c + 1) * per_tile)):
                edge = mine[j * tiles, pl.ds(r, own, stride=rows), :]
                if tiles > 1:
                    edge = jnp.where(lane < LANES // 2, edge,
                                     mine[j * tiles + tiles - 1, pl.ds(r, own, stride=rows), :])
                shift = 4 * (r - c * per_tile)
                if shift:
                    edge = pltpu.roll(edge, shift, 1)
                acc = jnp.where(((lane + (LANES + 2 - shift)) % LANES) < 4, edge, acc)
            col_send[j, c] = acc
    for side, picks in ((0, (0, 1)), (1, (rows - 2, rows - 1))):
        for j in range(groups):
            for i, r in enumerate(picks):
                for t in range(tiles):
                    row_send[side, j, i, :, t * LANES:(t + 1) * LANES] = mine[
                        j * tiles + t, pl.ds(r, own, stride=rows), :]
    for side, r in ((0, 0), (1, rows - 1)):
        for f in range(3):
            vrow_send[side, f:f + 1, :] = prim[0, f, r:r + 1, :]
        vrow_send[side, 3:4, :] = diff[r:r + 1, :]
        vrow_send[side, 4:8, :] = jnp.zeros((4, width), jnp.float32)
    vlane = lax.broadcasted_iota(jnp.int32, (rows, LANES), 1)
    left_acc = jnp.zeros((rows, LANES), jnp.float32)
    right_acc = jnp.zeros((rows, LANES), jnp.float32)
    for f in range(4):
        whole_field = prim[0, f] if f < 3 else diff[...]
        left = whole_field[:, :LANES]
        right = whole_field[:, width - LANES:]
        if f:
            left = pltpu.roll(left, f, 1)
            right = pltpu.roll(right, LANES - f, 1)
        left_acc = jnp.where(vlane == f, left, left_acc)
        right_acc = jnp.where(vlane == LANES - 1 - f, right, right_acc)
    vcol_send[0] = left_acc
    vcol_send[1] = right_acc

    for i, value in enumerate(coefficients([prim[1, f] for f in range(3)], diff[...])):
        coef1[i] = value

    pl.semaphore_wait(barrier, len(greeted))

    row_copies = []
    for side, dx in ((0, -1), (1, 1)):
        for k in range(groups):
            p = up(g, k + 1, groups)
            row_copies.append(send(row_send.at[side, p], row_land.at[side, g], rs_send.at[side, k],
                                   rs_recv.at[side, k], dev(p, up(x, dx, ranks), z)))
        row_copies.append(send(vrow_send.at[side], vrow_land.at[side], vr_send.at[side], vr_recv.at[side],
                               dev(g, up(x, dx, ranks), z)))
    chunk = z * groups + g
    chunks = spans * groups
    for side, step in ((0, -1), (1, 1)):
        to = up(chunk, step, chunks)
        row_copies.append(send(vcol_send.at[side], vcol_land.at[side], vc_send.at[side], vc_recv.at[side],
                               dev(lax.rem(to, groups), x, lax.div(to, groups))))
    for dx in (-1, 1, 0):
        slot = 1 - dx
        for j in range(groups):
            for side, step in ((0, -1), (1, 1)):
                dg = (j + step) % groups
                inside = 0 <= j + step < groups
                dz = z if inside else up(z, step, spans)

                def issue(j=j, side=side, dg=dg, dz=dz, slot=slot, dx=dx):
                    send(col_send.at[j], col_land.at[slot, side, g], cs_send.at[slot, side, j],
                         cs_recv.at[slot, side, g], dev(dg, up(x, dx, ranks), dz))
                if inside and dx == 0:
                    pl.when(g != dg)(issue)

                    @pl.when(g == dg)
                    def _(j=j, side=side, dg=dg, slot=slot):
                        col_land[slot, side, dg] = col_send[j]
                else:
                    issue()
    raw_copies = []
    for k in range(1, groups):
        p = up(g, k, groups)
        for t in range(tiles):
            raw_copies.append(send(
                tangent.at[:, pl.ds(pl.multiple_of(p * width + t * LANES, LANES), LANES)],
                land.at[t, pl.ds(pl.multiple_of(g * own * rows, 8), own * rows), :],
                raw_send.at[k, t], raw_recv.at[k, t], dev(p, x, z)))


    for copy in row_copies:
        copy.wait_recv()
    halo = []
    for f in range(4):
        after, before = vcol_land[0], vcol_land[1]
        if f:
            after = pltpu.roll(after, LANES - f, 1)
            before = pltpu.roll(before, f, 1)
        halo.append(jnp.where(vlane < LANES // 2, after, before))
    for i, value in enumerate(coefficients([prim[0, f] for f in range(3)], diff[...])):
        coef0[i, BLOCK:BLOCK + rows, :width] = value
    for i, value in enumerate(coefficients(halo[:3], halo[3])):
        coef0[i, BLOCK:BLOCK + rows, width:] = value
    for side, at in ((0, BLOCK + rows), (1, BLOCK - 1)):
        part = [vrow_land[side, f:f + 1, :] for f in range(4)]
        for i, value in enumerate(coefficients(part[:3], part[3])):
            coef0[i, at:at + 1, :width] = value
            coef0[i, at:at + 1, width:] = jnp.zeros((1, LANES), jnp.float32)

    for side, at in ((0, rows + 2), (1, 0)):
        for s in range(groups):
            for i in range(2):
                field[at + i, s * own:(s + 1) * own, :width] = row_land[side, s, i]

    other = dev(up(g, 1, groups), x, z)
    for slot in range(3):
        for side in range(2):
            for s in range(groups):
                def arrived(slot=slot, side=side, s=s):
                    pltpu.make_async_remote_copy(
                        src_ref=col_send.at[0], dst_ref=col_land.at[slot, side, s],
                        send_sem=cs_send.at[slot, side, 0], recv_sem=cs_recv.at[slot, side, s],
                        device_id=other, device_id_type=MESH).wait_recv()
                if slot == 1:
                    inside = (g < groups - 1) if side == 0 else (g > 0)
                    pl.when(jnp.logical_not(jnp.logical_and(inside, g == s)))(arrived)
                else:
                    arrived()
    for slot in range(3):
        for c in range(col_tiles):
            for s in range(groups):
                comb[slot, c, s * own:(s + 1) * own, :] = jnp.where(
                    lane % 4 < 2, col_land[slot, 0, s, c], col_land[slot, 1, s, c])

    def edge_tile(slot, r):
        shift = 4 * (r % per_tile)
        value = comb[slot, r // per_tile]
        return pltpu.roll(value, LANES - shift, 1) if shift else value

    nothing = jnp.zeros((dirs, LANES), jnp.float32)
    field[0, :, width:] = nothing
    field[rows + 3, :, width:] = nothing
    field[1, :, width:] = edge_tile(0, rows - 1)
    field[rows + 2, :, width:] = edge_tile(2, 0)
    for r in range(rows):
        field[r + 2, :, width:] = edge_tile(1, r)
    for copy in loads[base + 2:]:
        copy.wait()
    for copy in raw_copies:
        copy.wait_recv()
    for r in range(rows):
        for t in range(tiles):
            field[r + 2, :, t * LANES:(t + 1) * LANES] = land[t, pl.ds(r, dirs, stride=rows), :]

    def stencil(coef, before, centre, after):
        def spread(c):
            return jnp.broadcast_to(c, (dirs, c.shape[-1]))
        north = pltpu.roll(centre, wide - 1, 1)
        south = pltpu.roll(centre, 1, 1)
        keep = coef[0].shape[-1]
        return (spread(coef[0]) * after[:, :keep] + spread(coef[1]) * before[:, :keep]
                + spread(coef[2]) * north[:, :keep] + spread(coef[3]) * south[:, :keep]
                + spread(coef[4]) * centre[:, :keep])

    for r in (-1, rows):
        first[r + 1] = stencil([coef0[i, BLOCK + r:BLOCK + r + 1, :] for i in range(5)],
                               field[r + 1], field[r + 2], field[r + 3])

    def first_block(b, _):
        start = b * BLOCK
        coef = [coef0[i, pl.ds(start + BLOCK, BLOCK), :] for i in range(5)]
        for k in range(BLOCK):
            first[start + k + 1] = stencil([c[k:k + 1] for c in coef], field[start + k + 1],
                                           field[start + k + 2], field[start + k + 3])
        return 0

    for b in range(blocks):
        first_block(b, 0)

    stack = BLOCK * dirs

    def second_block(b, total):
        start = b * BLOCK
        coef = [coef1[i, pl.ds(start, BLOCK), :] for i in range(5)]
        for k in range(BLOCK):
            advanced[start + k] = stencil(
                [c[k:k + 1] for c in coef], first[start + k], first[start + k + 1], first[start + k + 2])
        part = advanced[pl.ds(start, BLOCK)].reshape(stack, width)
        return total + lax.dot_general(part, part, (((1,), (1,)), ((), ())), precision=HIGHEST,
                                       preferred_element_type=jnp.float32)

    total = jnp.zeros((stack, stack), jnp.float32)
    for b in range(blocks):
        total = second_block(b, total)
    si = lax.broadcasted_iota(jnp.int32, (stack, stack), 0)
    sj = lax.broadcasted_iota(jnp.int32, (stack, stack), 1)
    total = jnp.where(si // dirs == sj // dirs, total, 0.0)
    gram = total[:dirs]
    for k in range(1, BLOCK):
        gram = gram + total[k * dirs:(k + 1) * dirs]
    turn = stack // 2
    while turn >= dirs:
        gram = gram + pltpu.roll(gram, turn, 1)
        turn //= 2
    gl = lax.broadcasted_iota(jnp.int32, (dirs // 2, stack), 1) < stack // 2
    packed = jnp.where(gl, gram[:dirs // 2], gram[dirs // 2:])

    peers = groups * spans
    at1 = g * spans + z
    gram1[at1] = packed
    copies = []
    for k in range(1, peers):
        to = up(at1, k, peers)
        copies.append(send(gram1.at[at1], gram1.at[at1], g1_send.at[k], g1_recv.at[k],
                           dev(lax.div(to, spans), x, lax.rem(to, spans))))
    need = [min(dirs, -(-(p + 1) * own // BLOCK) * BLOCK) for p in range(groups)]
    soon = [min(blocks, blocks * dirs // (2 * need[p])) for p in range(groups)]

    def early(p, k, b):
        part = (pl.ds(b * BLOCK, BLOCK), pl.ds(0, need[p]), slice(None))
        return pltpu.make_async_remote_copy(
            src_ref=advanced.at[part], dst_ref=far.at[(k - 1, *part)], send_sem=early_send.at[k, b],
            recv_sem=early_recv.at[k, b], device_id=dev(up(g, k, groups), x, z), device_id_type=MESH)

    def late(p, k, b):
        spot = pl.ds(b * BLOCK, BLOCK)
        return pltpu.make_async_remote_copy(
            src_ref=result.at[pl.ds(p * own, own), spot, :],
            dst_ref=out.at[:, spot, pl.ds(pl.multiple_of(g * width, LANES), width)],
            send_sem=fin_send.at[k, b], recv_sem=fin_recv.at[k, b],
            device_id=dev(up(g, k, groups), x, z), device_id_type=MESH)

    def to_peers(act):
        for s in range(groups):
            @pl.when(g == s)
            def _(s=s):
                for k in range(1, groups):
                    act((s + k) % groups, k)

    @to_peers
    def _(p, k):
        for b in range(soon[p]):
            early(p, k, b).start()

    for copy in copies:
        copy.wait_recv()
    summed = gram1[0]
    for k in range(1, peers):
        summed = summed + gram1[k]
    gram2[x] = summed
    copies2 = []
    for k in range(1, ranks):
        copies2.append(send(gram2.at[x], gram2.at[x], g2_send.at[k], g2_recv.at[k],
                            dev(g, up(x, k, ranks), z)))
    for copy in copies2:
        copy.wait_recv()
    summed = gram2[0]
    for k in range(1, ranks):
        summed = summed + gram2[k]
    summed = summed * (1.0 / cells)
    turned = pltpu.roll(summed, stack // 2, 1)
    gram = jnp.concatenate([jnp.where(gl, summed, turned), jnp.where(gl, turned, summed)], axis=0)

    ri = lax.broadcasted_iota(jnp.int32, (dirs, stack), 0)
    rj = lax.broadcasted_iota(jnp.int32, (dirs, stack), 1)
    work = jnp.where(rj < dirs, gram, jnp.where(rj % dirs == ri, 1.0, 0.0))
    pivots = jnp.ones((dirs, stack), jnp.float32)
    spread_columns = [jnp.broadcast_to(work[:, k:k + 1], (dirs, stack)) for k in range(dirs)]
    for k in range(dirs):
        column = spread_columns[k]
        pivot = jnp.broadcast_to(column[k:k + 1], (dirs, stack))
        scaled = column * (1.0 / pivot)
        for j in range(k + 1, dirs):
            spread_columns[j] = spread_columns[j] - scaled * jnp.broadcast_to(column[j:j + 1], (dirs, stack))
        row = jnp.broadcast_to(work[k:k + 1], (dirs, stack))
        pivots = jnp.where(ri == k, pivot, pivots)
        work = jnp.where(ri > k, work - scaled * row, work)
    work = work * (1.0 / jnp.sqrt(pivots))
    factor[...] = jnp.where(rj >= ri, work, 0.0)[:, :dirs]
    inverse = jnp.where(rj < dirs, pltpu.roll(work, dirs, 1), work)
    mixer = jnp.concatenate([jnp.broadcast_to(inverse[d:d + 1], (BLOCK, stack)) for d in range(dirs)], axis=0)
    mixer = jnp.where(si % BLOCK == sj // dirs, mixer, 0.0)

    def mixed(p, block):
        return jnp.dot(mixer[p * own * BLOCK:(p + 1) * own * BLOCK], block.reshape(stack, width),
                       precision=HIGHEST, preferred_element_type=jnp.float32)

    @to_peers
    def _(p, k):
        for b in range(soon[p], blocks):
            value = mixed(p, advanced[b * BLOCK:(b + 1) * BLOCK])
            for d in range(own):
                result[p * own + d, b * BLOCK:(b + 1) * BLOCK, :] = value[d * BLOCK:(d + 1) * BLOCK]
            late(p, k, b).start()

    for p in range(groups):
        @pl.when(g == p)
        def _(p=p):
            def put(value, b, s):
                for d in range(own):
                    out[d, b * BLOCK:(b + 1) * BLOCK, s * width:(s + 1) * width] = value[d * BLOCK:(d + 1) * BLOCK]

            for b in range(blocks):
                put(mixed(p, advanced[b * BLOCK:(b + 1) * BLOCK]), b, p)
            for b in range(soon[p]):
                for k in range(1, groups):
                    early(p, k, b).wait_recv()
                    put(mixed(p, far[k - 1, b * BLOCK:(b + 1) * BLOCK]), b, (p - k) % groups)
            for b in range(soon[p], blocks):
                for k in range(1, groups):
                    late(p, k, b).wait_recv()

    @to_peers
    def _(p, k):
        for b in range(soon[p]):
            early(p, k, b).wait_send()
        for b in range(soon[p], blocks):
            late(p, k, b).wait_send()

    for copy in row_copies + raw_copies + copies + copies2:
        copy.wait_send()
    for dx in (-1, 1, 0):
        slot = 1 - dx
        for j in range(groups):
            for side, step in ((0, -1), (1, 1)):
                dg = (j + step) % groups

                def left(j=j, side=side, slot=slot):
                    pltpu.make_async_remote_copy(
                        src_ref=col_send.at[j], dst_ref=col_land.at[slot, side, g],
                        send_sem=cs_send.at[slot, side, j], recv_sem=cs_recv.at[slot, side, g],
                        device_id=other, device_id_type=MESH).wait_send()
                if 0 <= j + step < groups and dx == 0:
                    pl.when(g != dg)(left)
                else:
                    left()


def write_out(basis, factor, basis_out, factor_out, sem):
    copies = [pltpu.make_async_copy(basis, basis_out, sem.at[0]),
              pltpu.make_async_copy(factor, factor_out, sem.at[1])]
    for copy in copies:
        copy.start()
    for copy in copies:
        copy.wait()


def on_device(groups, ranks, spans, primal, tangent, diffusion):
    own, rows, columns = tangent.shape
    width = columns // groups
    tiles = width // LANES
    dirs = own * groups
    stack = BLOCK * dirs
    wide = width + LANES
    col_tiles = -(-rows // (LANES // 4))
    peers = groups * spans
    f32 = jnp.float32
    dma = pltpu.SemaphoreType.DMA
    hbm = pl.BlockSpec(memory_space=pl.ANY)
    vmem = pl.BlockSpec(memory_space=pltpu.VMEM)
    basis, factor = pl.pallas_call(
        functools.partial(kernel, groups, ranks, spans),
        out_shape=(pltpu.VMEM((own, rows, columns), f32), pltpu.VMEM((dirs, dirs), f32)),
        in_specs=[hbm, hbm, hbm],
        out_specs=(vmem, vmem),
        scratch_shapes=[
            pltpu.VMEM((groups * tiles, own * rows, LANES), f32),
            pltpu.VMEM((tiles, dirs * rows, LANES), f32),
            pltpu.VMEM(primal.shape, f32),
            pltpu.VMEM((rows, width), f32),
            pltpu.VMEM((2, groups, 2, own, width), f32),
            pltpu.VMEM((2, groups, 2, own, width), f32),
            pltpu.VMEM((groups, col_tiles, own, LANES), f32),
            pltpu.VMEM((3, 2, groups, col_tiles, own, LANES), f32),
            pltpu.VMEM((3, col_tiles, dirs, LANES), f32),
            pltpu.VMEM((2, rows, LANES), f32),
            pltpu.VMEM((2, rows, LANES), f32),
            pltpu.VMEM((2, 8, width), f32),
            pltpu.VMEM((2, 8, width), f32),
            pltpu.VMEM((rows + 4, dirs, wide), f32),
            pltpu.VMEM((rows + 2, dirs, wide), f32),
            pltpu.VMEM((5, rows + 2 * BLOCK, wide), f32),
            pltpu.VMEM((5, rows, width), f32),
            pltpu.VMEM((rows, dirs, width), f32),
            pltpu.VMEM((groups - 1, rows, dirs, width), f32),
            pltpu.VMEM((peers, dirs // 2, stack), f32),
            pltpu.VMEM((ranks, dirs // 2, stack), f32),
            pltpu.VMEM((dirs, rows, width), f32),
            dma((groups * tiles + 2 + tiles,)),
            dma((groups, tiles)), dma((groups, tiles)),
            dma((2, groups)), dma((2, groups)),
            dma((3, 2, groups)), dma((3, 2, groups)),
            dma((2,)), dma((2,)),
            dma((2,)), dma((2,)),
            dma((peers,)), dma((peers,)),
            dma((ranks,)), dma((ranks,)),
            dma((groups, rows // BLOCK)), dma((groups, rows // BLOCK)),
            dma((groups, rows // BLOCK)), dma((groups, rows // BLOCK)),
        ],
        compiler_params=pltpu.CompilerParams(collective_id=0, has_side_effects=True),
    )(primal, tangent.reshape(own * rows, columns), diffusion)
    return pl.pallas_call(
        write_out,
        out_shape=(jax.ShapeDtypeStruct(basis.shape, f32), jax.ShapeDtypeStruct(factor.shape, f32)),
        in_specs=[vmem, vmem],
        out_specs=(hbm, hbm),
        scratch_shapes=[dma((2,))],
    )(pltpu.with_memory_space_constraint(basis, pltpu.VMEM), pltpu.with_memory_space_constraint(factor, pltpu.VMEM))


def solution(mesh):
    sizes = dict(mesh.shape)
    in_specs = (P(None, None, "gx", ("gz", "grp")), P("grp", "gx", "gz"), P("gx", "gz"))
    out_specs = (P("grp", "gx", "gz"), P())
    return jax.shard_map(
        functools.partial(on_device, sizes["grp"], sizes["gx"], sizes["gz"]),
        mesh=mesh, in_specs=in_specs, out_specs=out_specs, check_vma=False)
```
